1024 devices in a mesh: tile: 64 (over x_hi, z), func: 16 (over y, x_lo, core).
Axes of the slice: x: 4 (x_hi: 2, x_lo: 2; x = x_hi * 2 + x_lo), y: 4, z: 32, core: 2. Of those that a mesh axis runs over, the one named last changes fastest.
Arguments:
- seeds: float32 [48, 5, 2048, 128], P('func', None, 'tile'), may hold values from -6 to 6
- checkpoints: float32 [2, 5, 2048, 128], P(None, None, ('tile', 'func')), may hold values from -0.6 to 4.2, as said below
Outputs:
- adjoint_start: float32 [48, 5, 2048, 128], P('func', None, 'tile')
The draws below stay inside these ranges and needn't reach their ends.
Inputs may be any that keep to these rules, and one draw needn't show every extreme that they name: `checkpoints`: each checkpoint cell is a state with density between 1 and 1.5, each velocity component between -0.4 and 0.4, and pressure between 1 and 1.5.
All inputs are finite; a program needn't handle non-finite values.
Results may differ from the reference program's by a relative error of at most 0.00002.
Values sent between devices are 32-bit elements; how exact they have to be, the bound alone decides.
A program may use at most 32 MiB of HBM per device.

```python
import jax
import jax.numpy as jnp
from jax import lax

CY = 32
NZ = 4
FIELDS = 5
STEPS = 2
NX = 2048
FUNCS = 48


def draw_checkpoints(key, part):
    shape = (STEPS, NX, CY * NZ)
    keys = jax.random.split(key, 5)
    density = jax.random.uniform(keys[0], shape, jnp.float32, 1.0, 1.5)
    speeds = [jnp.clip(0.15 * jax.random.normal(keys[1 + index], shape, jnp.float32), -0.4, 0.4) for index in range(3)]
    press = jax.random.uniform(keys[4], shape, jnp.float32, 1.0, 1.5)
    kinetic = 0.5 * density * (speeds[0] * speeds[0] + speeds[1] * speeds[1] + speeds[2] * speeds[2])
    energy = press / 0.4 + kinetic
    return jnp.stack([density, density * speeds[0], density * speeds[1], density * speeds[2], energy], axis=1)


def block_levels(key, shape, cuts, smallest, largest):
    gain, own = 1.0, jax.random.fold_in(key, 6)
    for dim, parts in cuts:
        heights = jnp.exp(jax.random.uniform(jax.random.fold_in(own, dim), (parts,), jnp.float32, smallest / len(cuts), largest / len(cuts)))
        gain = gain * jnp.repeat(heights, shape[dim] // parts).reshape([-1 if axis == dim else 1 for axis in range(len(shape))])
    return gain


def centred(rng, shape, scale, most, cuts=(), dtype=jnp.bfloat16):
    result = jax.random.normal(rng, shape, jnp.float32) * scale
    if len(cuts) > 0:
        result = block_levels(rng, shape, cuts, -0.22, 0.18) * result
    return jnp.clip(result, min=-most, max=most).astype(dtype)


def setup_inputs(seed: int = 0) -> dict:
    key_of = jax.random.split(jax.random.key(seed), 3)
    seeds = centred(key_of[0], (FUNCS, FIELDS, NX, CY * NZ), 1.0, 6.0, ((0, 16), (2, 64)), jnp.float32)
    checkpoints = draw_checkpoints(jax.random.fold_in(key_of[2], 71), 0)
    return {"seeds": seeds, "checkpoints": checkpoints}


step_size = 0.3

def diff_first(field):
    return (jnp.roll(field, 2, axis=-2) - jnp.roll(field, -2, axis=-2) + 8.0 * (jnp.roll(field, -1, axis=-2) - jnp.roll(field, 1, axis=-2))) / 12.0

def diff_second(field):
    return (jnp.roll(field, 2 * NZ, axis=-1) - jnp.roll(field, -2 * NZ, axis=-1) + 8.0 * (jnp.roll(field, -NZ, axis=-1) - jnp.roll(field, NZ, axis=-1))) / 12.0

def pressure(state):
    density, mom_x, mom_y, mom_z, energy = (state[0], state[1], state[2], state[3], state[4])
    return 0.4 * (energy - (mom_x * mom_x + mom_y * mom_y + mom_z * mom_z) / (2.0 * density))

def flux_first(state):
    density, mom_x, mom_y, mom_z, energy = (state[0], state[1], state[2], state[3], state[4])
    speed = mom_x / density
    press = pressure(state)
    return jnp.stack([mom_x, mom_x * speed + press, mom_y * speed, mom_z * speed, (energy + press) * speed])

def flux_second(state):
    density, mom_x, mom_y, mom_z, energy = (state[0], state[1], state[2], state[3], state[4])
    speed = mom_y / density
    press = pressure(state)
    return jnp.stack([mom_y, mom_x * speed, mom_y * speed + press, mom_z * speed, (energy + press) * speed])

def rhs_field(state):
    return -(diff_first(flux_first(state)) + diff_second(flux_second(state)))

def time_step(state):
    slope_one = rhs_field(state)
    slope_two = rhs_field(state + 0.5 * step_size * slope_one)
    slope_three = rhs_field(state + 0.5 * step_size * slope_two)
    slope_four = rhs_field(state + step_size * slope_three)
    return state + step_size / 6.0 * (slope_one + 2.0 * slope_two + 2.0 * slope_three + slope_four)

def reference(seeds, checkpoints):
    adjoint = seeds
    for moment in reversed(range(STEPS)):
        unused, pullback = jax.vjp(time_step, checkpoints[moment])

        def apply_one(single):
            return pullback(single)[0]
        adjoint = lax.map(apply_one, adjoint)
    return adjoint
```

```python
import functools

import jax
import jax.numpy as jnp
from jax import lax
from jax.experimental import pallas as pl
from jax.experimental.pallas import tpu as pltpu
from jax.sharding import PartitionSpec as P

NZ = 4
H = 0.3
L = 128
ROWS = 80
EDGE = 24
DEEP = (12, 20)
MESH = pl.DeviceIdType.MESH


def stencil_y(a):
    far = pltpu.roll(a, 2 * NZ, 1) - pltpu.roll(a, L - 2 * NZ, 1)
    near = pltpu.roll(a, L - NZ, 1) - pltpu.roll(a, NZ, 1)
    return far + 8.0 * near


def rowsat(lo, t, shift=0):
    return pl.ds(lo + shift + 8 * t, 8)


def loop(n, f, u):
    def step(i, c):
        for j in range(u):
            t = u * i + j
            if n % u:
                t = jnp.minimum(t, n - 1)
            f(t)
        return c

    lax.fori_loop(0, -(-n // u), step, 0)


def forward(load, u0, fx, base, coef, edge):
    scale = (0.5 * H / 12.0, 0.5 * H / 12.0, H / 12.0)

    def phase(k, lo, n):
        def tile(t):
            r = rowsat(lo, t)
            if k == 0:
                u = [load(c, lo, t) for c in range(5)]
                for c in range(5):
                    u0[c, r, :] = u[c]
            else:
                src, cst, u = fx.at[(k - 1) % 2], -scale[k - 1], []
                for c in range(5):
                    d = (src[c, rowsat(lo, t, -2), :] - src[c, rowsat(lo, t, 2), :]) + 8.0 * (
                        src[c, rowsat(lo, t, 1), :] - src[c, rowsat(lo, t, -1), :]
                    )
                    u.append(base[(k - 1) % 2, c, r, :] + cst * d)
            rho, mx, my, mz, en = u
            inv = 1.0 / rho
            vx, vy, vz = mx * inv, my * inv, mz * inv
            kin2 = mx * vx + my * vy + mz * vz
            p = 0.4 * (en - 0.5 * kin2)
            ep = en + p
            coef[k, 0, r, :] = vx
            coef[k, 1, r, :] = vy
            coef[k, 2, r, :] = vz
            coef[k, 3, r, :] = ep * inv
            coef[k, 4, r, :] = 0.5 * (kin2 * inv)
            if k < 3:
                fx[k % 2, 0, r, :] = mx
                fx[k % 2, 1, r, :] = mx * vx + p
                fx[k % 2, 2, r, :] = my * vx
                fx[k % 2, 3, r, :] = mz * vx
                fx[k % 2, 4, r, :] = ep * vx
                fy = (my, mx * vy, my * vy + p, mz * vy, ep * vy)
                start = u if k == 0 else [u0[c, r, :] for c in range(5)]
                for c in range(5):
                    base[k % 2, c, r, :] = start[c] - scale[k] * stencil_y(fy[c])

        loop(n, tile, 3)

    for k in range(4):
        lo = edge + 2 * k
        phase(k, lo, -(-(ROWS - 2 * lo) // 8))


def pull(w, f, coef, lo, t):
    a, b, mid = [], [], []
    for c in range(5):
        v = w[f, c, rowsat(lo, t), :]
        mid.append(v)
        a.append(
            (w[f, c, rowsat(lo, t, -2), :] - w[f, c, rowsat(lo, t, 2), :])
            + 8.0 * (w[f, c, rowsat(lo, t, 1), :] - w[f, c, rowsat(lo, t, -1), :])
        )
        b.append(stencil_y(v))
    vx, vy, vz, en, kin = coef
    s = a[1] * vx + a[2] * vy + a[3] * vz + a[4] * en
    q = b[1] * vx + b[2] * vy + b[3] * vz + b[4] * en
    e4 = a[4] * vx + b[4] * vy
    g = 0.4 * (a[1] + b[2] + e4)
    out = (
        kin * g - s * vx - q * vy,
        a[0] + s + a[1] * vx + b[1] * vy - g * vx,
        b[0] + q + a[2] * vx + b[2] * vy - g * vy,
        a[3] * vx + b[3] * vy - g * vz,
        e4 + g,
    )
    return mid, out


def backward(adj, w3, w2, w1, coef, first, store):
    near = 3.0 * H / 72.0
    plan = ((3, adj, w3, near), (2, w3, w2, near), (1, w2, w1, 2.0 * near), (0, w1, None, H / 72.0))
    for place, (k, src, dst, cst) in enumerate(plan):
        lo = first + 2 * place

        def tile(t, k=k, src=src, dst=dst, cst=cst, lo=lo):
            r = rowsat(lo, t)
            c5 = [coef[k, c, r, :] for c in range(5)]
            for f in range(3):
                mid, out = pull(src, f, c5, lo, t)
                for c in range(5):
                    start = mid[c] if k == 3 else adj[f, c, r, :]
                    if dst is not None:
                        dst[f, c, r, :] = start + cst * out[c]
                    else:
                        mix = (w3[f, c, r, :] + mid[c]) + 2.0 * w2[f, c, r, :] - start
                        store(f, c, lo, t, mix * (1.0 / 3.0) + cst * out[c])

        loop(-(-(ROWS - 2 * lo) // 8), tile, 1)


def kernel(tiles, funcs, seeds, chk, out, u0, fx, base, coef, adj, w3, w2, w1, st, own_sem, g_send, g_recv, z_send, z_recv):
    tile, func = lax.axis_index("tile"), lax.axis_index("func")
    up, down = lax.rem(tile + 1, tiles), lax.rem(tile + tiles - 1, tiles)

    def peer(d):
        return lax.rem(func + d, funcs)

    barrier = pltpu.get_barrier_semaphore()
    for d in range(1, funcs):
        pl.semaphore_signal(barrier, inc=1, device_id=(tile, peer(d)), device_id_type=MESH)
    for t in (up, down):
        pl.semaphore_signal(barrier, inc=1, device_id=(t, func), device_id_type=MESH)

    own_seeds = pltpu.make_async_copy(seeds, adj.at[:, :, pl.ds(EDGE, 32), :], own_sem.at[0])
    own_seeds.start()
    mine = EDGE // 2 + func
    own_state = [pltpu.make_async_copy(chk.at[s], st.at[s, :, mine], own_sem.at[1 + s]) for s in range(2)]
    for s in (1, 0):
        own_state[s].start()
    pl.semaphore_wait(barrier, funcs + 1)

    gather = [[], []]
    for s in (1, 0):
        for d in range(1, funcs):
            gather[s].append(
                pltpu.make_async_remote_copy(
                    src_ref=chk.at[s],
                    dst_ref=st.at[s, :, mine],
                    send_sem=g_send.at[s, d],
                    recv_sem=g_recv.at[s, d],
                    device_id=(tile, peer(d)),
                    device_id_type=MESH,
                )
            )
    def across(src, dst, slot, to):
        return pltpu.make_async_remote_copy(
            src_ref=src, dst_ref=dst, send_sem=z_send.at[slot], recv_sem=z_recv.at[slot],
            device_id=(to, func), device_id_type=MESH,
        )

    halo = [
        across(seeds.at[:, :, pl.ds(16, 16), :], adj.at[:, :, pl.ds(EDGE - 16, 16), :], 0, up),
        across(seeds.at[:, :, pl.ds(0, 16), :], adj.at[:, :, pl.ds(EDGE + 32, 16), :], 1, down),
    ]
    for copy in gather[1] + gather[0] + halo:
        copy.start()

    rims = [[], []]
    for s in (1, 0):
        n, lo, hi = DEEP[s] // 2, EDGE // 2, EDGE // 2 + 16
        own_state[s].wait()
        for copy in gather[s]:
            copy.wait_recv()
        rims[s] = [
            across(st.at[s, :, pl.ds(hi - n, n)], st.at[s, :, pl.ds(lo - n, n)], 2 + 2 * s, up),
            across(st.at[s, :, pl.ds(lo, n)], st.at[s, :, pl.ds(hi, n)], 3 + 2 * s, down),
        ]
        for copy in rims[s]:
            copy.start()

    def load(s):
        return lambda c, lo, t: st[s, c, pl.ds(lo // 2 + 4 * t, 4), :, :].reshape(8, L)

    for copy in rims[1]:
        copy.wait_recv()
    forward(load(1), u0, fx, base, coef, EDGE - DEEP[1])
    own_seeds.wait()
    for copy in halo:
        copy.wait_recv()

    def keep(f, c, lo, t, v):
        adj[f, c, rowsat(lo, t), :] = v

    backward(adj, w3, w2, w1, coef, EDGE - 14, keep)
    for copy in rims[0]:
        copy.wait_recv()
    forward(load(0), u0, fx, base, coef, EDGE - DEEP[0])

    def finish(f, c, lo, t, v):
        out[f, c, pl.ds(lo - EDGE + 8 * t, 8), :] = v

    backward(adj, w3, w2, w1, coef, EDGE - 6, finish)
    for copy in gather[1] + gather[0] + halo + rims[1] + rims[0]:
        copy.wait_send()


def solution(mesh):
    tiles, funcs = mesh.shape["tile"], mesh.shape["func"]

    def local(seeds, checkpoints):
        field = pltpu.VMEM((3, 5, ROWS, L), jnp.float32)
        return pl.pallas_call(
            functools.partial(kernel, tiles, funcs),
            out_shape=jax.ShapeDtypeStruct(seeds.shape, jnp.float32),
            in_specs=[pl.BlockSpec(memory_space=pl.ANY)] * 2,
            out_specs=pl.BlockSpec(memory_space=pltpu.VMEM),
            scratch_shapes=[
                pltpu.VMEM((5, ROWS, L), jnp.float32),
                pltpu.VMEM((2, 5, ROWS, L), jnp.float32),
                pltpu.VMEM((2, 5, ROWS, L), jnp.float32),
                pltpu.VMEM((4, 5, ROWS, L), jnp.float32),
                field,
                field,
                field,
                field,
                pltpu.VMEM((2, 5, ROWS // 2, 2, L), jnp.float32),
                pltpu.SemaphoreType.DMA((3,)),
                pltpu.SemaphoreType.DMA((2, 16)),
                pltpu.SemaphoreType.DMA((2, 16)),
                pltpu.SemaphoreType.DMA((6,)),
                pltpu.SemaphoreType.DMA((6,)),
            ],
            compiler_params=pltpu.CompilerParams(
                collective_id=0, has_side_effects=True, vmem_limit_bytes=16 * 2**20
            ),
        )(seeds, checkpoints)

    return jax.shard_map(
        local,
        mesh=mesh,
        in_specs=(P("func", None, "tile", None), P(None, None, ("tile", "func"), None)),
        out_specs=P("func", None, "tile", None),
        check_vma=False,
    )
```

```python
import functools

import jax
import jax.numpy as jnp
from jax import lax
from jax.experimental import pallas as pl
from jax.experimental.pallas import tpu as pltpu
from jax.sharding import PartitionSpec as P

NZ = 4
H = 0.3
L = 128
ROWS = 80
EDGE = 24
DEEP = (12, 20)
MESH = pl.DeviceIdType.MESH


def stencil_y(a):
    far = pltpu.roll(a, 2 * NZ, 1) - pltpu.roll(a, L - 2 * NZ, 1)
    near = pltpu.roll(a, L - NZ, 1) - pltpu.roll(a, NZ, 1)
    return far + 8.0 * near


def rowsat(row, shift=0):
    return pl.ds(row + shift, 8)


def sweep(lo, hi, f, u):
    n = (hi - lo + 7) // 8

    def step(i, c):
        for j in range(u):
            f(jnp.minimum(lo + 8 * (u * i + j), hi - 8))
        return c

    lax.fori_loop(0, (n + u - 1) // u, step, 0)


def forward(load, u0, fx, base, coef, span):
    scale = (0.5 * H / 12.0, 0.5 * H / 12.0, H / 12.0)

    def phase(k):
        def tile(row):
            r = rowsat(row)
            if k == 0:
                u = [load(c, row) for c in range(5)]
                for c in range(5):
                    u0[c, r, :] = u[c]
            else:
                src, cst, u = fx[k - 1], -scale[k - 1], []
                for c in range(5):
                    d = (src[c, rowsat(row, -2), :] - src[c, rowsat(row, 2), :]) + 8.0 * (
                        src[c, rowsat(row, 1), :] - src[c, rowsat(row, -1), :]
                    )
                    u.append(base[k - 1][c, r, :] + cst * d)
            rho, mx, my, mz, en = u
            inv = 1.0 / rho
            vx, vy, vz = mx * inv, my * inv, mz * inv
            kin2 = mx * vx + my * vy + mz * vz
            p = 0.4 * (en - 0.5 * kin2)
            ep = en + p
            coef[k, 0, r, :] = vx
            coef[k, 1, r, :] = vy
            coef[k, 2, r, :] = vz
            coef[k, 3, r, :] = ep * inv
            coef[k, 4, r, :] = 0.5 * (kin2 * inv)
            if k < 3:
                fx[k][0, r, :] = mx
                fx[k][1, r, :] = mx * vx + p
                fx[k][2, r, :] = my * vx
                fx[k][3, r, :] = mz * vx
                fx[k][4, r, :] = ep * vx
                fy = (my, mx * vy, my * vy + p, mz * vy, ep * vy)
                start = u if k == 0 else [u0[c, r, :] for c in range(5)]
                for c in range(5):
                    base[k][c, r, :] = start[c] - scale[k] * stencil_y(fy[c])

        lo, hi = span(k)
        sweep(lo, hi, tile, 3)

    for k in range(4):
        phase(k)


def pull(w, f, coef, row):
    a, b, mid = [], [], []
    for c in range(5):
        v = w[f, c, rowsat(row), :]
        mid.append(v)
        a.append(
            (w[f, c, rowsat(row, -2), :] - w[f, c, rowsat(row, 2), :])
            + 8.0 * (w[f, c, rowsat(row, 1), :] - w[f, c, rowsat(row, -1), :])
        )
        b.append(stencil_y(v))
    vx, vy, vz, en, kin = coef
    s = a[1] * vx + a[2] * vy + a[3] * vz + a[4] * en
    q = b[1] * vx + b[2] * vy + b[3] * vz + b[4] * en
    e4 = a[4] * vx + b[4] * vy
    g = 0.4 * (a[1] + b[2] + e4)
    out = (
        kin * g - s * vx - q * vy,
        a[0] + s + a[1] * vx + b[1] * vy - g * vx,
        b[0] + q + a[2] * vx + b[2] * vy - g * vy,
        a[3] * vx + b[3] * vy - g * vz,
        e4 + g,
    )
    return mid, out


def backward(adj, w3, w2, w1, coef, span, store):
    near = 3.0 * H / 72.0
    plan = ((3, adj, w3, near), (2, w3, w2, near), (1, w2, w1, 2.0 * near), (0, w1, None, H / 72.0))
    for place, (k, src, dst, cst) in enumerate(plan):

        def tile(row, k=k, src=src, dst=dst, cst=cst):
            r = rowsat(row)
            c5 = [coef[k, c, r, :] for c in range(5)]
            for f in range(3):
                mid, out = pull(src, f, c5, row)
                for c in range(5):
                    start = mid[c] if k == 3 else adj[f, c, r, :]
                    if dst is not None:
                        dst[f, c, r, :] = start + cst * out[c]
                    else:
                        mix = (w3[f, c, r, :] + mid[c]) + 2.0 * w2[f, c, r, :] - start
                        store(f, c, row, mix * (1.0 / 3.0) + cst * out[c])

        lo, hi = span(place)
        sweep(lo, hi, tile, 1)


def kernel(tiles, funcs, seeds, chk, out, *scratch):
    u0, fx, base = scratch[0:2], (scratch[2:5], scratch[5:8]), (scratch[8:11], scratch[11:14])
    coef, fields = scratch[14:16], scratch[16:24]
    st, own_sem, g_send, g_recv, z_send, z_recv = scratch[24:]
    tile, func = lax.axis_index("tile"), lax.axis_index("func")
    up, down = lax.rem(tile + 1, tiles), lax.rem(tile + tiles - 1, tiles)
    adj = fields[0]

    def peer(d):
        return lax.rem(func + d, funcs)

    barrier = pltpu.get_barrier_semaphore()
    for d in range(1, funcs):
        pl.semaphore_signal(barrier, inc=1, device_id=(tile, peer(d)), device_id_type=MESH)
    for t in (up, down):
        pl.semaphore_signal(barrier, inc=1, device_id=(t, func), device_id_type=MESH)

    mine = EDGE // 2 + func
    own_state = [pltpu.make_async_copy(chk.at[s], st.at[s, :, mine], own_sem.at[1 + s]) for s in range(2)]
    for s in (1, 0):
        own_state[s].start()
    own_seeds = pltpu.make_async_copy(seeds, adj.at[:, :, pl.ds(EDGE, 32), :], own_sem.at[0])
    own_seeds.start()
    pl.semaphore_wait(barrier, funcs + 1)

    gather = [
        [
            pltpu.make_async_remote_copy(
                src_ref=chk.at[s],
                dst_ref=st.at[s, :, mine],
                send_sem=g_send.at[s, d],
                recv_sem=g_recv.at[s, d],
                device_id=(tile, peer(d)),
                device_id_type=MESH,
            )
            for d in range(1, funcs)
        ]
        for s in range(2)
    ]

    def across(src, dst, slot, to):
        return pltpu.make_async_remote_copy(
            src_ref=src, dst_ref=dst, send_sem=z_send.at[slot], recv_sem=z_recv.at[slot],
            device_id=(to, func), device_id_type=MESH,
        )

    lo, hi = EDGE // 2, EDGE // 2 + 16
    rims = [
        (
            across(st.at[s, :, pl.ds(hi - n, n)], st.at[s, :, pl.ds(lo - n, n)], 2 + 2 * s, up),
            across(st.at[s, :, pl.ds(lo, n)], st.at[s, :, pl.ds(hi, n)], 3 + 2 * s, down),
        )
        for s, n in enumerate((DEEP[0] // 2, DEEP[1] // 2))
    ]
    halo = (
        across(seeds.at[:, :, pl.ds(16, 16), :], adj.at[:, :, pl.ds(EDGE - 16, 16), :], 0, up),
        across(seeds.at[:, :, pl.ds(0, 16), :], adj.at[:, :, pl.ds(EDGE + 32, 16), :], 1, down),
    )
    for copy in gather[1]:
        copy.start()
    for copy in halo:
        copy.start()

    def relay(s):
        own_state[s].wait()
        for copy in gather[s]:
            copy.wait_recv()
        for copy in rims[s]:
            copy.start()

    relay(1)
    for copy in gather[0]:
        copy.start()
    own_seeds.wait()

    def load(s):
        return lambda c, row: st[s, c, pl.ds(row // 2, 4), :, :].reshape(8, L)

    def part(g, carry):
        def only(want, copies):
            @pl.when(g == want)
            def _():
                for copy in copies:
                    copy.wait_recv()

        def region(below, above, low):
            return jnp.where(g == 0, EDGE + low, EDGE + below), jnp.where(g == 0, EDGE + above, EDGE + low)

        def sections(s):
            n = DEEP[s]
            return lambda k: region(2 * k - n, 32 + n - 2 * k, 2 * k)

        def stages(first):
            return lambda place: region(-16 + 2 * (first + place), 48 - 2 * (first + place), 4 + 2 * (first + place))

        only(0, (rims[1][1],))
        only(1, (rims[1][0], halo[0]))
        forward(load(1), u0[1], fx[1], base[1], coef[1], sections(1))

        @pl.when(g == 0)
        def _():
            relay(0)

        only(0, (halo[1],))

        def keep(f, c, row, v):
            fields[4][f, c, rowsat(row), :] = v

        backward(*fields[0:4], coef[1], stages(1), keep)
        only(0, (rims[0][1],))
        only(1, (rims[0][0],))
        forward(load(0), u0[0], fx[0], base[0], coef[0], sections(0))

        def finish(f, c, row, v):
            out[f, c, pl.ds(row - EDGE, 8), :] = v

        backward(*fields[4:8], coef[0], stages(5), finish)
        return carry

    lax.fori_loop(0, 2, part, 0)
    for copies in (*gather, halo, *rims):
        for copy in copies:
            copy.wait_send()


def solution(mesh):
    tiles, funcs = mesh.shape["tile"], mesh.shape["func"]

    def local(seeds, checkpoints):
        state = pltpu.VMEM((5, ROWS, L), jnp.float32)
        field = pltpu.VMEM((3, 5, ROWS, L), jnp.float32)
        return pl.pallas_call(
            functools.partial(kernel, tiles, funcs),
            out_shape=jax.ShapeDtypeStruct(seeds.shape, jnp.float32),
            in_specs=[pl.BlockSpec(memory_space=pltpu.HBM)] * 2,
            out_specs=pl.BlockSpec(memory_space=pltpu.VMEM),
            scratch_shapes=[state] * 14
            + [pltpu.VMEM((4, 5, ROWS, L), jnp.float32)] * 2
            + [field] * 8
            + [
                pltpu.VMEM((2, 5, ROWS // 2, 2, L), jnp.float32),
                pltpu.SemaphoreType.DMA((3,)),
                pltpu.SemaphoreType.DMA((2, 16)),
                pltpu.SemaphoreType.DMA((2, 16)),
                pltpu.SemaphoreType.DMA((6,)),
                pltpu.SemaphoreType.DMA((6,)),
            ],
            compiler_params=pltpu.CompilerParams(
                collective_id=0, has_side_effects=True, vmem_limit_bytes=16 * 2**20
            ),
        )(seeds, checkpoints)

    return jax.shard_map(
        local,
        mesh=mesh,
        in_specs=(P("func", None, "tile", None), P(None, None, ("tile", "func"), None)),
        out_specs=P("func", None, "tile", None),
        check_vma=False,
    )
```

```python
import functools

import jax
import jax.numpy as jnp
from jax import lax
from jax.experimental import pallas as pl
from jax.experimental.pallas import tpu as pltpu
from jax.sharding import PartitionSpec as P

NZ = 4
H = 0.3
L = 128
ROWS = 80
EDGE = 24
DEEP = (12, 20)
MESH = pl.DeviceIdType.MESH


def stencil_y(a):
    far = pltpu.roll(a, 2 * NZ, 1) - pltpu.roll(a, L - 2 * NZ, 1)
    near = pltpu.roll(a, L - NZ, 1) - pltpu.roll(a, NZ, 1)
    return far + 8.0 * near


def rowsat(row, shift=0):
    return pl.ds(row + shift, 8)


def sweep(lo, hi, f, u):
    n = (hi - lo + 7) // 8

    def step(i, c):
        for j in range(u):
            f(jnp.minimum(lo + 8 * (u * i + j), hi - 8))
        return c

    lax.fori_loop(0, (n + u - 1) // u, step, 0)


def forward(load, u0, fx, base, coef, span):
    scale = (0.5 * H / 12.0, 0.5 * H / 12.0, H / 12.0)

    def phase(k):
        def tile(row):
            r = rowsat(row)
            if k == 0:
                u = [load(c, row) for c in range(5)]
                for c in range(5):
                    u0[c, r, :] = u[c]
            else:
                src, cst, u = fx[k - 1], -scale[k - 1], []
                for c in range(5):
                    d = (src[c, rowsat(row, -2), :] - src[c, rowsat(row, 2), :]) + 8.0 * (
                        src[c, rowsat(row, 1), :] - src[c, rowsat(row, -1), :]
                    )
                    u.append(base[k - 1][c, r, :] + cst * d)
            rho, mx, my, mz, en = u
            inv = 1.0 / rho
            vx, vy, vz = mx * inv, my * inv, mz * inv
            kin2 = mx * vx + my * vy + mz * vz
            p = 0.4 * (en - 0.5 * kin2)
            ep = en + p
            coef[k, 0, r, :] = vx
            coef[k, 1, r, :] = vy
            coef[k, 2, r, :] = vz
            coef[k, 3, r, :] = ep * inv
            coef[k, 4, r, :] = 0.5 * (kin2 * inv)
            if k < 3:
                fx[k][0, r, :] = mx
                fx[k][1, r, :] = mx * vx + p
                fx[k][2, r, :] = my * vx
                fx[k][3, r, :] = mz * vx
                fx[k][4, r, :] = ep * vx
                fy = (my, mx * vy, my * vy + p, mz * vy, ep * vy)
                start = u if k == 0 else [u0[c, r, :] for c in range(5)]
                for c in range(5):
                    base[k][c, r, :] = start[c] - scale[k] * stencil_y(fy[c])

        lo, hi = span(k)
        sweep(lo, hi, tile, 3)

    for k in range(4):
        phase(k)


def pull(w, f, coef, row):
    a, b, mid = [], [], []
    for c in range(5):
        v = w[f, c, rowsat(row), :]
        mid.append(v)
        a.append(
            (w[f, c, rowsat(row, -2), :] - w[f, c, rowsat(row, 2), :])
            + 8.0 * (w[f, c, rowsat(row, 1), :] - w[f, c, rowsat(row, -1), :])
        )
        b.append(stencil_y(v))
    vx, vy, vz, en, kin = coef
    s = a[1] * vx + a[2] * vy + a[3] * vz + a[4] * en
    q = b[1] * vx + b[2] * vy + b[3] * vz + b[4] * en
    e4 = a[4] * vx + b[4] * vy
    g = 0.4 * (a[1] + b[2] + e4)
    out = (
        kin * g - s * vx - q * vy,
        a[0] + s + a[1] * vx + b[1] * vy - g * vx,
        b[0] + q + a[2] * vx + b[2] * vy - g * vy,
        a[3] * vx + b[3] * vy - g * vz,
        e4 + g,
    )
    return mid, out


def backward(adj, w3, w2, w1, coef, span, store):
    near = 3.0 * H / 72.0
    plan = ((3, adj, w3, near), (2, w3, w2, near), (1, w2, w1, 2.0 * near), (0, w1, None, H / 72.0))
    for place, (k, src, dst, cst) in enumerate(plan):

        def tile(row, k=k, src=src, dst=dst, cst=cst):
            r = rowsat(row)
            c5 = [coef[k, c, r, :] for c in range(5)]
            for f in range(3):
                mid, out = pull(src, f, c5, row)
                for c in range(5):
                    start = mid[c] if k == 3 else adj[f, c, r, :]
                    if dst is not None:
                        dst[f, c, r, :] = start + cst * out[c]
                    else:
                        mix = (w3[f, c, r, :] + mid[c]) + 2.0 * w2[f, c, r, :] - start
                        store(f, c, row, mix * (1.0 / 3.0) + cst * out[c])

        lo, hi = span(place)
        sweep(lo, hi, tile, 1)


def kernel(tiles, funcs, seeds, chk, out, *scratch):
    u0, fx, base = scratch[0:2], (scratch[2:5], scratch[5:8]), (scratch[8:11], scratch[11:14])
    coef, fields = scratch[14:16], scratch[16:24]
    st, own_sem, g_send, g_recv, z_send, z_recv, entered = scratch[24:]
    tile, func = lax.axis_index("tile"), lax.axis_index("func")
    up, down = lax.rem(tile + 1, tiles), lax.rem(tile + tiles - 1, tiles)
    adj = fields[0]
    bottom = lax.rem(tile, tiles // 2) == 0
    top = lax.rem(tile, tiles // 2) == tiles // 2 - 1

    def peer(d):
        return lax.rem(func + d, funcs)

    barrier = pltpu.get_barrier_semaphore()
    for d in range(1, funcs):
        pl.semaphore_signal(barrier, inc=1, device_id=(tile, peer(d)), device_id_type=MESH)
    pl.semaphore_signal(barrier, inc=1, device_id=(down, func), device_id_type=MESH)

    @pl.when(jnp.logical_not(top))
    def _():
        pl.semaphore_signal(barrier, inc=1, device_id=(up, func), device_id_type=MESH)


    mine = EDGE // 2 + func
    own_state = [pltpu.make_async_copy(chk.at[s], st.at[s, :, mine], own_sem.at[1 + s]) for s in range(2)]
    for s in (1, 0):
        own_state[s].start()
    own_seeds = pltpu.make_async_copy(seeds, adj.at[:, :, pl.ds(EDGE, 32), :], own_sem.at[0])
    own_seeds.start()
    pl.semaphore_wait(barrier, funcs + 1 - bottom.astype(jnp.int32))

    @pl.when(top)
    def _():
        pl.semaphore_signal(entered, inc=1, device_id=(up, func), device_id_type=MESH)

    gather = [
        [
            pltpu.make_async_remote_copy(
                src_ref=chk.at[s],
                dst_ref=st.at[s, :, mine],
                send_sem=g_send.at[s, d],
                recv_sem=g_recv.at[s, d],
                device_id=(tile, peer(d)),
                device_id_type=MESH,
            )
            for d in range(1, funcs)
        ]
        for s in range(2)
    ]

    def across(src, dst, slot, to):
        return pltpu.make_async_remote_copy(
            src_ref=src, dst_ref=dst, send_sem=z_send.at[slot], recv_sem=z_recv.at[slot],
            device_id=(to, func), device_id_type=MESH,
        )

    lo, hi = EDGE // 2, EDGE // 2 + 16
    rims = [
        (
            across(st.at[s, :, pl.ds(hi - n, n)], st.at[s, :, pl.ds(lo - n, n)], 2 + 2 * s, up),
            across(st.at[s, :, pl.ds(lo, n)], st.at[s, :, pl.ds(hi, n)], 3 + 2 * s, down),
        )
        for s, n in enumerate((DEEP[0] // 2, DEEP[1] // 2))
    ]
    halo = (
        across(seeds.at[:, :, pl.ds(16, 16), :], adj.at[:, :, pl.ds(EDGE - 16, 16), :], 0, up),
        across(seeds.at[:, :, pl.ds(0, 16), :], adj.at[:, :, pl.ds(EDGE + 32, 16), :], 1, down),
    )
    for copy in gather[1]:
        copy.start()

    def launch(pair):
        pair[0].start()

        @pl.when(jnp.logical_not(bottom))
        def _():
            pair[1].start()

    launch(halo)

    def relay(s):
        own_state[s].wait()
        for copy in gather[s]:
            copy.wait_recv()
        launch(rims[s])

    relay(1)
    for copy in gather[0]:
        copy.start()
    own_seeds.wait()

    def load(s):
        return lambda c, row: st[s, c, pl.ds(row // 2, 4), :, :].reshape(8, L)

    def part(g, carry):
        above = (g == 0) != top

        def arrive(pair):
            @pl.when(above)
            def _():
                pair[1].wait_recv()

            @pl.when(jnp.logical_not(above))
            def _():
                pair[0].wait_recv()

        def region(deep, rim):
            first, last = -deep, 32 + deep
            low = jnp.where(top, jnp.where(g == 0, first, 32 - rim), jnp.where(g == 0, rim, first))
            high = jnp.where(top, jnp.where(g == 0, 32 - rim, last), jnp.where(g == 0, last, rim))
            return EDGE + low, EDGE + high

        def sections(s):
            return lambda k: region(DEEP[s] - 2 * k, 2 * k)

        def stages(first):
            return lambda place: region(16 - 2 * (first + place), 4 + 2 * (first + place))

        arrive(rims[1])
        forward(load(1), u0[1], fx[1], base[1], coef[1], sections(1))

        @pl.when(g == 0)
        def _():
            relay(0)

        arrive(halo)

        def keep(f, c, row, v):
            fields[4][f, c, rowsat(row), :] = v

        backward(*fields[0:4], coef[1], stages(1), keep)
        arrive(rims[0])
        forward(load(0), u0[0], fx[0], base[0], coef[0], sections(0))

        def finish(f, c, row, v):
            out[f, c, pl.ds(row - EDGE, 8), :] = v

        backward(*fields[4:8], coef[0], stages(5), finish)

        @pl.when(jnp.logical_and(g == 0, bottom))
        def _():
            pl.semaphore_wait(entered, 1)
            for pair in (halo, rims[1], rims[0]):
                pair[1].start()

        return carry

    lax.fori_loop(0, 2, part, 0)
    for copies in (*gather, halo, *rims):
        for copy in copies:
            copy.wait_send()


def solution(mesh):
    tiles, funcs = mesh.shape["tile"], mesh.shape["func"]

    def local(seeds, checkpoints):
        state = pltpu.VMEM((5, ROWS, L), jnp.float32)
        field = pltpu.VMEM((3, 5, ROWS, L), jnp.float32)
        return pl.pallas_call(
            functools.partial(kernel, tiles, funcs),
            out_shape=jax.ShapeDtypeStruct(seeds.shape, jnp.float32),
            in_specs=[pl.BlockSpec(memory_space=pltpu.HBM)] * 2,
            out_specs=pl.BlockSpec(memory_space=pltpu.VMEM),
            scratch_shapes=[state] * 14
            + [pltpu.VMEM((4, 5, ROWS, L), jnp.float32)] * 2
            + [field] * 8
            + [
                pltpu.VMEM((2, 5, ROWS // 2, 2, L), jnp.float32),
                pltpu.SemaphoreType.DMA((3,)),
                pltpu.SemaphoreType.DMA((2, 16)),
                pltpu.SemaphoreType.DMA((2, 16)),
                pltpu.SemaphoreType.DMA((6,)),
                pltpu.SemaphoreType.DMA((6,)),
                pltpu.SemaphoreType.REGULAR,
            ],
            compiler_params=pltpu.CompilerParams(
                collective_id=0, has_side_effects=True, vmem_limit_bytes=16 * 2**20
            ),
        )(seeds, checkpoints)

    return jax.shard_map(
        local,
        mesh=mesh,
        in_specs=(P("func", None, "tile", None), P(None, None, ("tile", "func"), None)),
        out_specs=P("func", None, "tile", None),
        check_vma=False,
    )
```

```python
import functools

import jax
import jax.numpy as jnp
from jax import lax
from jax.experimental import pallas as pl
from jax.experimental.pallas import tpu as pltpu
from jax.sharding import PartitionSpec as P

NZ = 4
H = 0.3
L = 128
ROWS = 80
EDGE = 24
DEEP = (12, 20)
MESH = pl.DeviceIdType.MESH


def y_matrix():
    gap = (lax.broadcasted_iota(jnp.int32, (L, L), 0) - lax.broadcasted_iota(jnp.int32, (L, L), 1) + L) % L
    near = jnp.where(gap == NZ, 8.0, jnp.where(gap == L - NZ, -8.0, 0.0))
    return near + jnp.where(gap == L - 2 * NZ, 1.0, jnp.where(gap == 2 * NZ, -1.0, 0.0))


def along_y(v, mat):
    high = v.astype(jnp.bfloat16)
    low = (v - high.astype(jnp.float32)).astype(jnp.bfloat16)
    return jnp.dot(high, mat, preferred_element_type=jnp.float32) + jnp.dot(low, mat, preferred_element_type=jnp.float32)


def rowsat(row, shift=0):
    return pl.ds(row + shift, 8)


def sweep(lo, hi, f, u):
    n = (hi - lo + 7) // 8

    def step(i, c):
        f([jnp.minimum(lo + 8 * (u * i + j), hi - 8) for j in range(u)])
        return c

    lax.fori_loop(0, (n + u - 1) // u, step, 0)


def forward(load, fx, base, coef, span, mat):
    scale = (0.5 * H / 12.0, 0.5 * H / 12.0, H / 12.0)

    def phase(k):
        def tile(row):
            r = rowsat(row)
            if k == 0:
                u = [load(c, row) for c in range(5)]
            else:
                src, cst, u = fx[k - 1], -scale[k - 1], []
                for c in range(5):
                    d = (src[c, rowsat(row, -2), :] - src[c, rowsat(row, 2), :]) + 8.0 * (
                        src[c, rowsat(row, 1), :] - src[c, rowsat(row, -1), :]
                    )
                    u.append(base[k - 1][c, r, :] + cst * d)
            rho, mx, my, mz, en = u
            inv = 1.0 / rho
            vx, vy, vz = mx * inv, my * inv, mz * inv
            kin2 = mx * vx + my * vy + mz * vz
            p = 0.4 * (en - 0.5 * kin2)
            ep = en + p
            coef[k, 0, r, :] = vx
            coef[k, 1, r, :] = vy
            coef[k, 2, r, :] = vz
            coef[k, 3, r, :] = ep * inv
            coef[k, 4, r, :] = 0.5 * (kin2 * inv)
            if k == 3:
                return []
            fx[k][0, r, :] = mx
            fx[k][1, r, :] = mx * vx + p
            fx[k][2, r, :] = my * vx
            fx[k][3, r, :] = mz * vx
            fx[k][4, r, :] = ep * vx
            return [my, mx * vy, my * vy + p, mz * vy, ep * vy]

        def tiles(rows):
            fy = [flux for row in rows for flux in tile(row)]
            if k == 3:
                return
            slope = scale[k] * along_y(jnp.concatenate(fy, axis=0), mat[...])
            for j, row in enumerate(rows):
                for c in range(5):
                    at = 8 * (5 * j + c)
                    base[k][c, rowsat(row), :] = load(c, row) - slope[at : at + 8]

        lo, hi = span(k)
        sweep(lo, hi, tiles, 3)

    for k in range(4):
        phase(k)


def pull(w, f, coef, row, b):
    a = []
    for c in range(5):
        a.append(
            (w[f, c, rowsat(row, -2), :] - w[f, c, rowsat(row, 2), :])
            + 8.0 * (w[f, c, rowsat(row, 1), :] - w[f, c, rowsat(row, -1), :])
        )
    vx, vy, vz, en, kin = coef
    s = a[1] * vx + a[2] * vy + a[3] * vz + a[4] * en
    q = b[1] * vx + b[2] * vy + b[3] * vz + b[4] * en
    e4 = a[4] * vx + b[4] * vy
    g = 0.4 * (a[1] + b[2] + e4)
    return (
        kin * g - s * vx - q * vy,
        a[0] + s + a[1] * vx + b[1] * vy - g * vx,
        b[0] + q + a[2] * vx + b[2] * vy - g * vy,
        a[3] * vx + b[3] * vy - g * vz,
        e4 + g,
    )


def backward(adj, w3, w2, w1, coef, span, store, mat):
    near = 3.0 * H / 72.0
    plan = ((3, adj, w3, near), (2, w3, w2, near), (1, w2, w1, 2.0 * near), (0, w1, None, H / 72.0))
    for place, (k, src, dst, cst) in enumerate(plan):

        def tile(rows, k=k, src=src, dst=dst, cst=cst):
            mid = [src[f, c, rowsat(row), :] for row in rows for f in range(3) for c in range(5)]
            along = along_y(jnp.concatenate(mid, axis=0), mat[...])
            for j, row in enumerate(rows):
                r = rowsat(row)
                c5 = [coef[k, c, r, :] for c in range(5)]
                for f in range(3):
                    first = 5 * (3 * j + f)
                    out = pull(src, f, c5, row, [along[8 * (first + c) : 8 * (first + c) + 8] for c in range(5)])
                    for c in range(5):
                        start = mid[first + c] if k == 3 else adj[f, c, r, :]
                        if dst is not None:
                            dst[f, c, r, :] = start + cst * out[c]
                        else:
                            mix = (w3[f, c, r, :] + src[f, c, r, :]) + 2.0 * w2[f, c, r, :] - start
                            store(f, c, row, mix * (1.0 / 3.0) + cst * out[c])

        lo, hi = span(place)
        sweep(lo, hi, tile, 1)


def kernel(tiles, funcs, seeds, chk, out, *scratch):
    fx, base = (scratch[0:3], scratch[3:6]), (scratch[6:9], scratch[9:12])
    coef, fields = scratch[12:14], scratch[14:22]
    st, own_sem, g_send, g_recv, z_send, z_recv, entered, mat = scratch[22:]
    tile, func = lax.axis_index("tile"), lax.axis_index("func")
    up, down = lax.rem(tile + 1, tiles), lax.rem(tile + tiles - 1, tiles)
    adj = fields[0]
    bottom = lax.rem(tile, tiles // 2) == 0
    top = lax.rem(tile, tiles // 2) == tiles // 2 - 1

    def peer(d):
        return lax.rem(func + d, funcs)

    barrier = pltpu.get_barrier_semaphore()
    for d in range(1, funcs):
        pl.semaphore_signal(barrier, inc=1, device_id=(tile, peer(d)), device_id_type=MESH)
    pl.semaphore_signal(barrier, inc=1, device_id=(down, func), device_id_type=MESH)

    @pl.when(jnp.logical_not(top))
    def _():
        pl.semaphore_signal(barrier, inc=1, device_id=(up, func), device_id_type=MESH)


    mine = EDGE // 2 + func
    own_state = [pltpu.make_async_copy(chk.at[s], st.at[s, :, pl.ds(2 * mine, 2), :], own_sem.at[1 + s]) for s in range(2)]
    for s in (1, 0):
        own_state[s].start()
    own_seeds = pltpu.make_async_copy(seeds, adj.at[:, :, pl.ds(EDGE, 32), :], own_sem.at[0])
    own_seeds.start()
    mat[...] = y_matrix().astype(jnp.bfloat16)
    pl.semaphore_wait(barrier, funcs + 1 - bottom.astype(jnp.int32))

    @pl.when(top)
    def _():
        pl.semaphore_signal(entered, inc=1, device_id=(up, func), device_id_type=MESH)

    gather = [
        [
            pltpu.make_async_remote_copy(
                src_ref=chk.at[s],
                dst_ref=st.at[s, :, pl.ds(2 * mine, 2), :],
                send_sem=g_send.at[s, d],
                recv_sem=g_recv.at[s, d],
                device_id=(tile, peer(d)),
                device_id_type=MESH,
            )
            for d in range(1, funcs)
        ]
        for s in range(2)
    ]

    def across(src, dst, slot, to):
        return pltpu.make_async_remote_copy(
            src_ref=src, dst_ref=dst, send_sem=z_send.at[slot], recv_sem=z_recv.at[slot],
            device_id=(to, func), device_id_type=MESH,
        )

    lo, hi = EDGE // 2, EDGE // 2 + 16
    rims = [
        (
            across(st.at[s, :, pl.ds(2 * (hi - n), 2 * n), :], st.at[s, :, pl.ds(2 * (lo - n), 2 * n), :], 2 + 2 * s, up),
            across(st.at[s, :, pl.ds(2 * lo, 2 * n), :], st.at[s, :, pl.ds(2 * hi, 2 * n), :], 3 + 2 * s, down),
        )
        for s, n in enumerate((DEEP[0] // 2, DEEP[1] // 2))
    ]
    halo = (
        across(seeds.at[:, :, pl.ds(16, 16), :], adj.at[:, :, pl.ds(EDGE - 16, 16), :], 0, up),
        across(seeds.at[:, :, pl.ds(0, 16), :], adj.at[:, :, pl.ds(EDGE + 32, 16), :], 1, down),
    )
    for copy in gather[1]:
        copy.start()

    def launch(pair):
        pair[0].start()

        @pl.when(jnp.logical_not(bottom))
        def _():
            pair[1].start()

    launch(halo)

    def relay(s):
        own_state[s].wait()
        for copy in gather[s]:
            copy.wait_recv()
        launch(rims[s])

    relay(1)
    for copy in gather[0]:
        copy.start()
    own_seeds.wait()

    def load(s):
        return lambda c, row: st[s, c, rowsat(row), :]

    def part(g, carry):
        above = (g == 0) != top

        def arrive(pair):
            @pl.when(above)
            def _():
                pair[1].wait_recv()

            @pl.when(jnp.logical_not(above))
            def _():
                pair[0].wait_recv()

        def region(deep, rim):
            first, last = -deep, 32 + deep
            low = jnp.where(top, jnp.where(g == 0, first, 32 - rim), jnp.where(g == 0, rim, first))
            high = jnp.where(top, jnp.where(g == 0, 32 - rim, last), jnp.where(g == 0, last, rim))
            return EDGE + low, EDGE + high

        def sections(s):
            return lambda k: region(DEEP[s] - 2 * k, 2 * k)

        def stages(first):
            return lambda place: region(16 - 2 * (first + place), 4 + 2 * (first + place))

        arrive(rims[1])
        forward(load(1), fx[1], base[1], coef[1], sections(1), mat)

        @pl.when(g == 0)
        def _():
            relay(0)

        arrive(halo)

        def keep(f, c, row, v):
            fields[4][f, c, rowsat(row), :] = v

        backward(*fields[0:4], coef[1], stages(1), keep, mat)
        arrive(rims[0])
        forward(load(0), fx[0], base[0], coef[0], sections(0), mat)

        def finish(f, c, row, v):
            out[f, c, pl.ds(row - EDGE, 8), :] = v

        backward(*fields[4:8], coef[0], stages(5), finish, mat)

        @pl.when(jnp.logical_and(g == 0, bottom))
        def _():
            pl.semaphore_wait(entered, 1)
            for pair in (halo, rims[1], rims[0]):
                pair[1].start()

        return carry

    lax.fori_loop(0, 2, part, 0)
    for copies in (*gather, halo, *rims):
        for copy in copies:
            copy.wait_send()


def solution(mesh):
    tiles, funcs = mesh.shape["tile"], mesh.shape["func"]

    def local(seeds, checkpoints):
        state = pltpu.VMEM((5, ROWS, L), jnp.float32)
        field = pltpu.VMEM((3, 5, ROWS, L), jnp.float32)
        return pl.pallas_call(
            functools.partial(kernel, tiles, funcs),
            out_shape=jax.ShapeDtypeStruct(seeds.shape, jnp.float32),
            in_specs=[pl.BlockSpec(memory_space=pltpu.HBM)] * 2,
            out_specs=pl.BlockSpec(memory_space=pltpu.VMEM),
            scratch_shapes=[state] * 12
            + [pltpu.VMEM((4, 5, ROWS, L), jnp.float32)] * 2
            + [field] * 8
            + [
                pltpu.VMEM((2, 5, ROWS, L), jnp.float32),
                pltpu.SemaphoreType.DMA((3,)),
                pltpu.SemaphoreType.DMA((2, 16)),
                pltpu.SemaphoreType.DMA((2, 16)),
                pltpu.SemaphoreType.DMA((6,)),
                pltpu.SemaphoreType.DMA((6,)),
                pltpu.SemaphoreType.REGULAR,
                pltpu.VMEM((L, L), jnp.bfloat16),
            ],
            compiler_params=pltpu.CompilerParams(
                collective_id=0, has_side_effects=True, vmem_limit_bytes=16 * 2**20
            ),
        )(seeds, checkpoints)

    return jax.shard_map(
        local,
        mesh=mesh,
        in_specs=(P("func", None, "tile", None), P(None, None, ("tile", "func"), None)),
        out_specs=P("func", None, "tile", None),
        check_vma=False,
    )
```

```python
import functools

import jax
import jax.numpy as jnp
from jax import lax
from jax.experimental import pallas as pl
from jax.experimental.pallas import tpu as pltpu
from jax.sharding import PartitionSpec as P

NZ = 4
H = 0.3
L = 128
ROWS = 80
EDGE = 24
DEEP = (12, 20)
MESH = pl.DeviceIdType.MESH


def y_matrix():
    gap = (lax.broadcasted_iota(jnp.int32, (L, L), 0) - lax.broadcasted_iota(jnp.int32, (L, L), 1) + L) % L
    near = jnp.where(gap == NZ, 8.0, jnp.where(gap == L - NZ, -8.0, 0.0))
    return near + jnp.where(gap == L - 2 * NZ, 1.0, jnp.where(gap == 2 * NZ, -1.0, 0.0))


def along_y(v, mat):
    high = v.astype(jnp.bfloat16)
    low = (v - high.astype(jnp.float32)).astype(jnp.bfloat16)
    return jnp.dot(high, mat, preferred_element_type=jnp.float32) + jnp.dot(low, mat, preferred_element_type=jnp.float32)


def rolled_y(a):
    far = pltpu.roll(a, 2 * NZ, 1) - pltpu.roll(a, L - 2 * NZ, 1)
    near = pltpu.roll(a, L - NZ, 1) - pltpu.roll(a, NZ, 1)
    return far + 8.0 * near


def rowsat(row, shift=0):
    return pl.ds(row + shift, 8)


def sweep(lo, hi, f, u):
    n = (hi - lo + 7) // 8

    def step(i, c):
        f([jnp.minimum(lo + 8 * (u * i + j), hi - 8) for j in range(u)])
        return c

    lax.fori_loop(0, (n + u - 1) // u, step, 0)


def forward(load, fx, base, coef, span):
    scale = (0.5 * H / 12.0, 0.5 * H / 12.0, H / 12.0)

    def phase(k):
        def tile(row):
            r = rowsat(row)
            if k == 0:
                u = [load(c, row) for c in range(5)]
            else:
                src, cst, u = fx[k - 1], -scale[k - 1], []
                for c in range(5):
                    d = (src[c, rowsat(row, -2), :] - src[c, rowsat(row, 2), :]) + 8.0 * (
                        src[c, rowsat(row, 1), :] - src[c, rowsat(row, -1), :]
                    )
                    u.append(base[k - 1][c, r, :] + cst * d)
            rho, mx, my, mz, en = u
            inv = 1.0 / rho
            vx, vy, vz = mx * inv, my * inv, mz * inv
            kin2 = mx * vx + my * vy + mz * vz
            p = 0.4 * (en - 0.5 * kin2)
            ep = en + p
            coef[k, 0, r, :] = vx
            coef[k, 1, r, :] = vy
            coef[k, 2, r, :] = vz
            coef[k, 3, r, :] = ep * inv
            coef[k, 4, r, :] = 0.5 * (kin2 * inv)
            if k == 3:
                return []
            fx[k][0, r, :] = mx
            fx[k][1, r, :] = mx * vx + p
            fx[k][2, r, :] = my * vx
            fx[k][3, r, :] = mz * vx
            fx[k][4, r, :] = ep * vx
            return [my, mx * vy, my * vy + p, mz * vy, ep * vy]

        def tiles(rows):
            for row in rows:
                for c, flux in enumerate(tile(row)):
                    base[k][c, rowsat(row), :] = load(c, row) - scale[k] * rolled_y(flux)

        lo, hi = span(k)
        sweep(lo, hi, tiles, 3)

    for k in range(4):
        phase(k)


def pull(w, f, coef, row, b):
    a = []
    for c in range(5):
        a.append(
            (w[f, c, rowsat(row, -2), :] - w[f, c, rowsat(row, 2), :])
            + 8.0 * (w[f, c, rowsat(row, 1), :] - w[f, c, rowsat(row, -1), :])
        )
    vx, vy, vz, en, kin = coef
    s = a[1] * vx + a[2] * vy + a[3] * vz + a[4] * en
    q = b[1] * vx + b[2] * vy + b[3] * vz + b[4] * en
    e4 = a[4] * vx + b[4] * vy
    g = 0.4 * (a[1] + b[2] + e4)
    return (
        kin * g - s * vx - q * vy,
        a[0] + s + a[1] * vx + b[1] * vy - g * vx,
        b[0] + q + a[2] * vx + b[2] * vy - g * vy,
        a[3] * vx + b[3] * vy - g * vz,
        e4 + g,
    )


def backward(adj, w3, w2, w1, coef, span, store, mat):
    near = 3.0 * H / 72.0
    plan = ((3, adj, w3, near), (2, w3, w2, near), (1, w2, w1, 2.0 * near), (0, w1, None, H / 72.0))
    for place, (k, src, dst, cst) in enumerate(plan):

        def tile(rows, k=k, src=src, dst=dst, cst=cst):
            mid = [src[f, c, rowsat(row), :] for row in rows for f in range(3) for c in range(5)]
            along = along_y(jnp.concatenate(mid, axis=0), mat[...])
            for j, row in enumerate(rows):
                r = rowsat(row)
                c5 = [coef[k, c, r, :] for c in range(5)]
                for f in range(3):
                    first = 5 * (3 * j + f)
                    out = pull(src, f, c5, row, [along[8 * (first + c) : 8 * (first + c) + 8] for c in range(5)])
                    for c in range(5):
                        start = mid[first + c] if k == 3 else adj[f, c, r, :]
                        if dst is not None:
                            dst[f, c, r, :] = start + cst * out[c]
                        else:
                            mix = (w3[f, c, r, :] + src[f, c, r, :]) + 2.0 * w2[f, c, r, :] - start
                            store(f, c, row, mix * (1.0 / 3.0) + cst * out[c])

        lo, hi = span(place)
        sweep(lo, hi, tile, 4)


def kernel(tiles, funcs, seeds, chk, out, *scratch):
    fx, base = (scratch[0:3], scratch[3:6]), (scratch[6:9], scratch[9:12])
    coef, fields = scratch[12:14], scratch[14:22]
    st, own_sem, g_send, g_recv, z_send, z_recv, entered, mat = scratch[22:]
    tile, func = lax.axis_index("tile"), lax.axis_index("func")
    up, down = lax.rem(tile + 1, tiles), lax.rem(tile + tiles - 1, tiles)
    adj = fields[0]
    bottom = lax.rem(tile, tiles // 2) == 0
    top = lax.rem(tile, tiles // 2) == tiles // 2 - 1

    def peer(d):
        return lax.rem(func + d, funcs)

    barrier = pltpu.get_barrier_semaphore()
    for d in range(1, funcs):
        pl.semaphore_signal(barrier, inc=1, device_id=(tile, peer(d)), device_id_type=MESH)
    pl.semaphore_signal(barrier, inc=1, device_id=(down, func), device_id_type=MESH)

    @pl.when(jnp.logical_not(top))
    def _():
        pl.semaphore_signal(barrier, inc=1, device_id=(up, func), device_id_type=MESH)


    mine = EDGE // 2 + func
    own_state = [pltpu.make_async_copy(chk.at[s], st.at[s, :, pl.ds(2 * mine, 2), :], own_sem.at[1 + s]) for s in range(2)]
    for s in (1, 0):
        own_state[s].start()
    own_seeds = pltpu.make_async_copy(seeds, adj.at[:, :, pl.ds(EDGE, 32), :], own_sem.at[0])
    own_seeds.start()
    mat[...] = y_matrix().astype(jnp.bfloat16)
    pl.semaphore_wait(barrier, funcs + 1 - bottom.astype(jnp.int32))

    @pl.when(top)
    def _():
        pl.semaphore_signal(entered, inc=1, device_id=(up, func), device_id_type=MESH)

    gather = [
        [
            pltpu.make_async_remote_copy(
                src_ref=chk.at[s],
                dst_ref=st.at[s, :, pl.ds(2 * mine, 2), :],
                send_sem=g_send.at[s, d],
                recv_sem=g_recv.at[s, d],
                device_id=(tile, peer(d)),
                device_id_type=MESH,
            )
            for d in range(1, funcs)
        ]
        for s in range(2)
    ]

    def across(src, dst, slot, to):
        return pltpu.make_async_remote_copy(
            src_ref=src, dst_ref=dst, send_sem=z_send.at[slot], recv_sem=z_recv.at[slot],
            device_id=(to, func), device_id_type=MESH,
        )

    lo, hi = EDGE // 2, EDGE // 2 + 16
    rims = [
        (
            across(st.at[s, :, pl.ds(2 * (hi - n), 2 * n), :], st.at[s, :, pl.ds(2 * (lo - n), 2 * n), :], 2 + 2 * s, up),
            across(st.at[s, :, pl.ds(2 * lo, 2 * n), :], st.at[s, :, pl.ds(2 * hi, 2 * n), :], 3 + 2 * s, down),
        )
        for s, n in enumerate((DEEP[0] // 2, DEEP[1] // 2))
    ]
    halo = (
        across(seeds.at[:, :, pl.ds(16, 16), :], adj.at[:, :, pl.ds(EDGE - 16, 16), :], 0, up),
        across(seeds.at[:, :, pl.ds(0, 16), :], adj.at[:, :, pl.ds(EDGE + 32, 16), :], 1, down),
    )
    for copy in gather[1]:
        copy.start()

    def launch(pair):
        pair[0].start()

        @pl.when(jnp.logical_not(bottom))
        def _():
            pair[1].start()

    launch(halo)

    def relay(s):
        own_state[s].wait()
        for copy in gather[s]:
            copy.wait_recv()
        launch(rims[s])

    relay(1)
    for copy in gather[0]:
        copy.start()
    own_seeds.wait()

    def load(s):
        return lambda c, row: st[s, c, rowsat(row), :]

    def part(g, carry):
        above = (g == 0) != top

        def arrive(pair):
            @pl.when(above)
            def _():
                pair[1].wait_recv()

            @pl.when(jnp.logical_not(above))
            def _():
                pair[0].wait_recv()

        def region(deep, rim):
            first, last = -deep, 32 + deep
            low = jnp.where(top, jnp.where(g == 0, first, 32 - rim), jnp.where(g == 0, rim, first))
            high = jnp.where(top, jnp.where(g == 0, 32 - rim, last), jnp.where(g == 0, last, rim))
            return EDGE + low, EDGE + high

        def sections(s):
            return lambda k: region(DEEP[s] - 2 * k, 2 * k)

        def stages(first):
            return lambda place: region(16 - 2 * (first + place), 4 + 2 * (first + place))

        arrive(rims[1])
        forward(load(1), fx[1], base[1], coef[1], sections(1))

        @pl.when(g == 0)
        def _():
            relay(0)

        arrive(halo)

        def keep(f, c, row, v):
            fields[4][f, c, rowsat(row), :] = v

        backward(*fields[0:4], coef[1], stages(1), keep, mat)
        arrive(rims[0])
        forward(load(0), fx[0], base[0], coef[0], sections(0))

        def finish(f, c, row, v):
            out[f, c, pl.ds(row - EDGE, 8), :] = v

        backward(*fields[4:8], coef[0], stages(5), finish, mat)

        @pl.when(jnp.logical_and(g == 0, bottom))
        def _():
            pl.semaphore_wait(entered, 1)
            for pair in (halo, rims[1], rims[0]):
                pair[1].start()

        return carry

    lax.fori_loop(0, 2, part, 0)
    for copies in (*gather, halo, *rims):
        for copy in copies:
            copy.wait_send()


def solution(mesh):
    tiles, funcs = mesh.shape["tile"], mesh.shape["func"]

    def local(seeds, checkpoints):
        state = pltpu.VMEM((5, ROWS, L), jnp.float32)
        field = pltpu.VMEM((3, 5, ROWS, L), jnp.float32)
        return pl.pallas_call(
            functools.partial(kernel, tiles, funcs),
            out_shape=jax.ShapeDtypeStruct(seeds.shape, jnp.float32),
            in_specs=[pl.BlockSpec(memory_space=pltpu.HBM)] * 2,
            out_specs=pl.BlockSpec(memory_space=pltpu.VMEM),
            scratch_shapes=[state] * 12
            + [pltpu.VMEM((4, 5, ROWS, L), jnp.float32)] * 2
            + [field] * 8
            + [
                pltpu.VMEM((2, 5, ROWS, L), jnp.float32),
                pltpu.SemaphoreType.DMA((3,)),
                pltpu.SemaphoreType.DMA((2, 16)),
                pltpu.SemaphoreType.DMA((2, 16)),
                pltpu.SemaphoreType.DMA((6,)),
                pltpu.SemaphoreType.DMA((6,)),
                pltpu.SemaphoreType.REGULAR,
                pltpu.VMEM((L, L), jnp.bfloat16),
            ],
            compiler_params=pltpu.CompilerParams(
                collective_id=0, has_side_effects=True, vmem_limit_bytes=16 * 2**20
            ),
        )(seeds, checkpoints)

    return jax.shard_map(
        local,
        mesh=mesh,
        in_specs=(P("func", None, "tile", None), P(None, None, ("tile", "func"), None)),
        out_specs=P("func", None, "tile", None),
        check_vma=False,
    )
```

```python
import functools

import jax
import jax.numpy as jnp
from jax import lax
from jax.experimental import pallas as pl
from jax.experimental.pallas import tpu as pltpu
from jax.sharding import PartitionSpec as P

NZ = 4
H = 0.3
L = 128
ROWS = 80
EDGE = 24
DEEP = (12, 20)
MESH = pl.DeviceIdType.MESH


def y_matrix():
    gap = (lax.broadcasted_iota(jnp.int32, (L, L), 0) - lax.broadcasted_iota(jnp.int32, (L, L), 1) + L) % L
    near = jnp.where(gap == NZ, 8.0, jnp.where(gap == L - NZ, -8.0, 0.0))
    return near + jnp.where(gap == L - 2 * NZ, 1.0, jnp.where(gap == 2 * NZ, -1.0, 0.0))


def along_y(v, mat):
    high = v.astype(jnp.bfloat16)
    low = (v - high.astype(jnp.float32)).astype(jnp.bfloat16)
    return jnp.dot(high, mat, preferred_element_type=jnp.float32) + jnp.dot(low, mat, preferred_element_type=jnp.float32)


def rolled_y(a):
    far = pltpu.roll(a, 2 * NZ, 1) - pltpu.roll(a, L - 2 * NZ, 1)
    near = pltpu.roll(a, L - NZ, 1) - pltpu.roll(a, NZ, 1)
    return far + 8.0 * near


def rowsat(row, shift=0):
    return pl.ds(row + shift, 8)


def sweep(lo, hi, f, u):
    n = (hi - lo + 7) // 8

    def step(i, c):
        f([jnp.minimum(lo + 8 * (u * i + j), hi - 8) for j in range(u)])
        return c

    lax.fori_loop(0, (n + u - 1) // u, step, 0)


def forward(load, fx, base, coef, span):
    scale = (0.5 * H / 12.0, 0.5 * H / 12.0, H / 12.0)

    def phase(k):
        def tile(row):
            r = rowsat(row)
            if k == 0:
                u = [load(c, row) for c in range(5)]
            else:
                src, cst, u = fx[k - 1], -scale[k - 1], []
                for c in range(5):
                    d = (src[c, rowsat(row, -2), :] - src[c, rowsat(row, 2), :]) + 8.0 * (
                        src[c, rowsat(row, 1), :] - src[c, rowsat(row, -1), :]
                    )
                    u.append(base[k - 1][c, r, :] + cst * d)
            rho, mx, my, mz, en = u
            inv = 1.0 / rho
            vx, vy, vz = mx * inv, my * inv, mz * inv
            kin2 = mx * vx + my * vy + mz * vz
            p = 0.4 * (en - 0.5 * kin2)
            ep = en + p
            coef[k, 0, r, :] = vx
            coef[k, 1, r, :] = vy
            coef[k, 2, r, :] = vz
            coef[k, 3, r, :] = ep * inv
            coef[k, 4, r, :] = 0.5 * (kin2 * inv)
            if k == 3:
                return []
            fx[k][0, r, :] = mx
            fx[k][1, r, :] = mx * vx + p
            fx[k][2, r, :] = my * vx
            fx[k][3, r, :] = mz * vx
            fx[k][4, r, :] = ep * vx
            return [my, mx * vy, my * vy + p, mz * vy, ep * vy]

        def tiles(rows):
            for row in rows:
                for c, flux in enumerate(tile(row)):
                    base[k][c, rowsat(row), :] = load(c, row) - scale[k] * rolled_y(flux)

        lo, hi = span(k)
        sweep(lo, hi, tiles, 3)

    for k in range(4):
        phase(k)


def pull(w, f, coef, row, b):
    a = []
    for c in range(5):
        a.append(
            (w[f, c, rowsat(row, -2), :] - w[f, c, rowsat(row, 2), :])
            + 8.0 * (w[f, c, rowsat(row, 1), :] - w[f, c, rowsat(row, -1), :])
        )
    vx, vy, vz, en, kin = coef
    s = a[1] * vx + a[2] * vy + a[3] * vz + a[4] * en
    q = b[1] * vx + b[2] * vy + b[3] * vz + b[4] * en
    e4 = a[4] * vx + b[4] * vy
    g = 0.4 * (a[1] + b[2] + e4)
    return (
        kin * g - s * vx - q * vy,
        a[0] + s + a[1] * vx + b[1] * vy - g * vx,
        b[0] + q + a[2] * vx + b[2] * vy - g * vy,
        a[3] * vx + b[3] * vy - g * vz,
        e4 + g,
    )


def backward(adj, w3, w2, w1, coef, span, store, mat):
    near = 3.0 * H / 72.0
    plan = ((3, adj, w3, near), (2, w3, w2, near), (1, w2, w1, 2.0 * near), (0, w1, None, H / 72.0))
    for place, (k, src, dst, cst) in enumerate(plan):

        def tile(rows, k=k, src=src, dst=dst, cst=cst):
            mid = [src[f, c, rowsat(row), :] for row in rows for f in range(3) for c in range(5)]
            along = along_y(jnp.concatenate(mid, axis=0), mat[...])
            for j, row in enumerate(rows):
                r = rowsat(row)
                c5 = [coef[k, c, r, :] for c in range(5)]
                for f in range(3):
                    first = 5 * (3 * j + f)
                    out = pull(src, f, c5, row, [along[8 * (first + c) : 8 * (first + c) + 8] for c in range(5)])
                    for c in range(5):
                        start = mid[first + c] if k == 3 else adj[f, c, r, :]
                        if dst is not None:
                            dst[f, c, r, :] = start + cst * out[c]
                        else:
                            mix = (w3[f, c, r, :] + src[f, c, r, :]) + 2.0 * w2[f, c, r, :] - start
                            store(f, c, row, mix * (1.0 / 3.0) + cst * out[c])

        lo, hi = span(place)
        sweep(lo, hi, tile, 4)


def kernel(tiles, funcs, seeds, chk, out, *scratch):
    fx, base = (scratch[0:3], scratch[3:6]), (scratch[6:9], scratch[9:12])
    coef, fields = scratch[12:14], scratch[14:22]
    st, own_sem, g_send, g_recv, z_send, z_recv, entered, mat = scratch[22:]
    tile, func = lax.axis_index("tile"), lax.axis_index("func")
    up, down = lax.rem(tile + 1, tiles), lax.rem(tile + tiles - 1, tiles)
    adj = fields[0]
    bottom = lax.rem(tile, tiles // 2) == 0
    top = lax.rem(tile, tiles // 2) == tiles // 2 - 1

    def peer(d):
        return lax.rem(func + d, funcs)

    barrier = pltpu.get_barrier_semaphore()
    for d in range(1, funcs):
        pl.semaphore_signal(barrier, inc=1, device_id=(tile, peer(d)), device_id_type=MESH)
    pl.semaphore_signal(barrier, inc=1, device_id=(down, func), device_id_type=MESH)

    @pl.when(jnp.logical_not(top))
    def _():
        pl.semaphore_signal(barrier, inc=1, device_id=(up, func), device_id_type=MESH)


    mine = EDGE // 2 + func
    own_state = [pltpu.make_async_copy(chk.at[s], st.at[s, :, pl.ds(2 * mine, 2), :], own_sem.at[1 + s]) for s in range(2)]
    for s in (1, 0):
        own_state[s].start()
    own_seeds = pltpu.make_async_copy(seeds, adj.at[:, :, pl.ds(EDGE, 32), :], own_sem.at[0])
    own_seeds.start()
    mat[...] = y_matrix().astype(jnp.bfloat16)
    pl.semaphore_wait(barrier, funcs + 1 - bottom.astype(jnp.int32))

    @pl.when(top)
    def _():
        pl.semaphore_signal(entered, inc=1, device_id=(up, func), device_id_type=MESH)

    gather = [
        [
            pltpu.make_async_remote_copy(
                src_ref=chk.at[s],
                dst_ref=st.at[s, :, pl.ds(2 * mine, 2), :],
                send_sem=g_send.at[s, d],
                recv_sem=g_recv.at[s, d],
                device_id=(tile, peer(d)),
                device_id_type=MESH,
            )
            for d in range(1, funcs)
        ]
        for s in range(2)
    ]

    def across(src, dst, slot, to):
        return pltpu.make_async_remote_copy(
            src_ref=src, dst_ref=dst, send_sem=z_send.at[slot], recv_sem=z_recv.at[slot],
            device_id=(to, func), device_id_type=MESH,
        )

    lo, hi = EDGE // 2, EDGE // 2 + 16
    rims = [
        (
            across(st.at[s, :, pl.ds(2 * (hi - n), 2 * n), :], st.at[s, :, pl.ds(2 * (lo - n), 2 * n), :], 2 + 2 * s, up),
            across(st.at[s, :, pl.ds(2 * lo, 2 * n), :], st.at[s, :, pl.ds(2 * hi, 2 * n), :], 3 + 2 * s, down),
        )
        for s, n in enumerate((DEEP[0] // 2, DEEP[1] // 2))
    ]
    halo = (
        across(seeds.at[:, :, pl.ds(16, 16), :], adj.at[:, :, pl.ds(EDGE - 16, 16), :], 0, up),
        across(seeds.at[:, :, pl.ds(0, 16), :], adj.at[:, :, pl.ds(EDGE + 32, 16), :], 1, down),
    )
    for copy in gather[1]:
        copy.start()

    def launch(pair):
        pair[0].start()

        @pl.when(jnp.logical_not(bottom))
        def _():
            pair[1].start()

    launch(halo)

    def relay(s):
        own_state[s].wait()
        for copy in gather[s]:
            copy.wait_recv()
        launch(rims[s])

    relay(1)
    for copy in gather[0]:
        copy.start()
    own_seeds.wait()

    def load(s):
        return lambda c, row: st[s, c, rowsat(row), :]

    def part(g, carry):
        above = (g == 0) != top

        def arrive(pair):
            @pl.when(above)
            def _():
                pair[1].wait_recv()

            @pl.when(jnp.logical_not(above))
            def _():
                pair[0].wait_recv()

        def region(deep, rim):
            first, last = -deep, 32 + deep
            low = jnp.where(top, jnp.where(g == 0, first, 32 - rim), jnp.where(g == 0, rim, first))
            high = jnp.where(top, jnp.where(g == 0, 32 - rim, last), jnp.where(g == 0, last, rim))
            return EDGE + low, EDGE + high

        def sections(s):
            return lambda k: region(DEEP[s] - 2 * k, 2 * k)

        def stages(first):
            return lambda place: region(16 - 2 * (first + place), 4 + 2 * (first + place))

        arrive(rims[1])
        forward(load(1), fx[1], base[1], coef[1], sections(1))

        @pl.when(g == 0)
        def _():
            relay(0)

        arrive(halo)

        def keep(f, c, row, v):
            fields[4][f, c, rowsat(row), :] = v

        backward(*fields[0:4], coef[1], stages(1), keep, mat)
        arrive(rims[0])
        forward(load(0), fx[0], base[0], coef[0], sections(0))

        def finish(f, c, row, v):
            out[f, c, pl.ds(row - EDGE, 8), :] = v

        backward(*fields[4:8], coef[0], stages(5), finish, mat)

        @pl.when(jnp.logical_and(g == 0, bottom))
        def _():
            pl.semaphore_wait(entered, 1)
            for pair in (halo, rims[1], rims[0]):
                pair[1].start()

        return carry

    lax.fori_loop(0, 2, part, 0)
    for copies in (*gather, halo, *rims):
        for copy in copies:
            copy.wait_send()


def solution(mesh):
    tiles, funcs = mesh.shape["tile"], mesh.shape["func"]

    def local(seeds, checkpoints):
        state = pltpu.VMEM((5, ROWS, L), jnp.float32)
        field = pltpu.VMEM((3, 5, ROWS, L), jnp.float32)
        return pl.pallas_call(
            functools.partial(kernel, tiles, funcs),
            out_shape=jax.ShapeDtypeStruct(seeds.shape, jnp.float32),
            in_specs=[pl.BlockSpec(memory_space=pltpu.HBM)] * 2,
            out_specs=pl.BlockSpec(memory_space=pltpu.VMEM),
            scratch_shapes=[state] * 12
            + [pltpu.VMEM((4, 5, ROWS, L), jnp.float32)] * 2
            + [field] * 8
            + [
                pltpu.VMEM((2, 5, ROWS, L), jnp.float32),
                pltpu.SemaphoreType.DMA((3,)),
                pltpu.SemaphoreType.DMA((2, 16)),
                pltpu.SemaphoreType.DMA((2, 16)),
                pltpu.SemaphoreType.DMA((6,)),
                pltpu.SemaphoreType.DMA((6,)),
                pltpu.SemaphoreType.REGULAR,
                pltpu.VMEM((L, L), jnp.bfloat16),
            ],
            compiler_params=pltpu.CompilerParams(
                collective_id=0, has_side_effects=True, vmem_limit_bytes=60_000_000
            ),
        )(seeds, checkpoints)

    return jax.shard_map(
        local,
        mesh=mesh,
        in_specs=(P("func", None, "tile", None), P(None, None, ("tile", "func"), None)),
        out_specs=P("func", None, "tile", None),
        check_vma=False,
    )
```

```python
import functools

import jax
import jax.numpy as jnp
from jax import lax
from jax.experimental import pallas as pl
from jax.experimental.pallas import tpu as pltpu
from jax.sharding import PartitionSpec as P

NZ = 4
H = 0.3
L = 128
ROWS = 80
EDGE = 24
DEEP = (12, 20)
MESH = pl.DeviceIdType.MESH


def y_matrix():
    gap = (lax.broadcasted_iota(jnp.int32, (L, L), 0) - lax.broadcasted_iota(jnp.int32, (L, L), 1) + L) % L
    near = jnp.where(gap == NZ, 8.0, jnp.where(gap == L - NZ, -8.0, 0.0))
    return near + jnp.where(gap == L - 2 * NZ, 1.0, jnp.where(gap == 2 * NZ, -1.0, 0.0))


def along_y(v, mat):
    high = v.astype(jnp.bfloat16)
    low = (v - high.astype(jnp.float32)).astype(jnp.bfloat16)
    return jnp.dot(high, mat, preferred_element_type=jnp.float32) + jnp.dot(low, mat, preferred_element_type=jnp.float32)


def rolled_y(a):
    far = pltpu.roll(a, 2 * NZ, 1) - pltpu.roll(a, L - 2 * NZ, 1)
    near = pltpu.roll(a, L - NZ, 1) - pltpu.roll(a, NZ, 1)
    return far + 8.0 * near


def rowsat(row, shift=0):
    return pl.ds(row + shift, 8)


def sweep(lo, hi, f, u):
    n = (hi - lo + 7) // 8

    def step(i, c):
        f([jnp.minimum(lo + 8 * (u * i + j), hi - 8) for j in range(u)])
        return c

    lax.fori_loop(0, (n + u - 1) // u, step, 0)


def forward(load, fx, base, coef, span):
    scale = (0.5 * H / 12.0, 0.5 * H / 12.0, H / 12.0)

    def phase(k):
        def tile(row):
            r = rowsat(row)
            if k == 0:
                u = [load(c, row) for c in range(5)]
            else:
                src, cst, u = fx[k - 1], -scale[k - 1], []
                for c in range(5):
                    d = (src[c, rowsat(row, -2), :] - src[c, rowsat(row, 2), :]) + 8.0 * (
                        src[c, rowsat(row, 1), :] - src[c, rowsat(row, -1), :]
                    )
                    u.append(base[k - 1][c, r, :] + cst * d)
            rho, mx, my, mz, en = u
            inv = 1.0 / rho
            vx, vy, vz = mx * inv, my * inv, mz * inv
            kin2 = mx * vx + my * vy + mz * vz
            p = 0.4 * (en - 0.5 * kin2)
            ep = en + p
            coef[k, 0, r, :] = vx
            coef[k, 1, r, :] = vy
            coef[k, 2, r, :] = vz
            coef[k, 3, r, :] = ep * inv
            coef[k, 4, r, :] = 0.5 * (kin2 * inv)
            if k == 3:
                return []
            fx[k][0, r, :] = mx
            fx[k][1, r, :] = mx * vx + p
            fx[k][2, r, :] = my * vx
            fx[k][3, r, :] = mz * vx
            fx[k][4, r, :] = ep * vx
            return [my, mx * vy, my * vy + p, mz * vy, ep * vy]

        def tiles(rows):
            for row in rows:
                for c, flux in enumerate(tile(row)):
                    base[k][c, rowsat(row), :] = load(c, row) - scale[k] * rolled_y(flux)

        lo, hi = span(k)
        sweep(lo, hi, tiles, 3)

    for k in range(4):
        phase(k)


def pull(w, f, coef, row, b):
    a = []
    for c in range(5):
        a.append(
            (w[f, c, rowsat(row, -2), :] - w[f, c, rowsat(row, 2), :])
            + 8.0 * (w[f, c, rowsat(row, 1), :] - w[f, c, rowsat(row, -1), :])
        )
    vx, vy, vz, en, kin = coef
    s = a[1] * vx + a[2] * vy + a[3] * vz + a[4] * en
    q = b[1] * vx + b[2] * vy + b[3] * vz + b[4] * en
    e4 = a[4] * vx + b[4] * vy
    g = 0.4 * (a[1] + b[2] + e4)
    return (
        kin * g - s * vx - q * vy,
        a[0] + s + a[1] * vx + b[1] * vy - g * vx,
        b[0] + q + a[2] * vx + b[2] * vy - g * vy,
        a[3] * vx + b[3] * vy - g * vz,
        e4 + g,
    )


def backward(adj, w3, w2, w1, coef, span, store, mat):
    near = 3.0 * H / 72.0
    plan = ((3, adj, w3, near), (2, w3, w2, near), (1, w2, w1, 2.0 * near), (0, w1, None, H / 72.0))
    for place, (k, src, dst, cst) in enumerate(plan):

        def tile(rows, k=k, src=src, dst=dst, cst=cst):
            mid = [src[f, c, rowsat(row), :] for row in rows for f in range(3) for c in range(5)]
            along = along_y(jnp.concatenate(mid, axis=0), mat[...])
            for j, row in enumerate(rows):
                r = rowsat(row)
                c5 = [coef[k, c, r, :] for c in range(5)]
                for f in range(3):
                    first = 5 * (3 * j + f)
                    out = pull(src, f, c5, row, [along[8 * (first + c) : 8 * (first + c) + 8] for c in range(5)])
                    for c in range(5):
                        start = mid[first + c] if k == 3 else adj[f, c, r, :]
                        if dst is not None:
                            dst[f, c, r, :] = start + cst * out[c]
                        else:
                            mix = (w3[f, c, r, :] + src[f, c, r, :]) + 2.0 * w2[f, c, r, :] - start
                            store(f, c, row, mix * (1.0 / 3.0) + cst * out[c])

        lo, hi = span(place)
        sweep(lo, hi, tile, 4)


def kernel(tiles, funcs, seeds, chk, out, *scratch):
    fx, base = (scratch[0:3], scratch[3:6]), (scratch[6:9], scratch[9:12])
    coef, fields = scratch[12:14], scratch[14:22]
    st, own_sem, g_send, g_recv, z_send, z_recv, entered, mat = scratch[22:]
    tile, func = lax.axis_index("tile"), lax.axis_index("func")
    up, down = lax.rem(tile + 1, tiles), lax.rem(tile + tiles - 1, tiles)
    adj = fields[0]
    bottom = lax.rem(tile, tiles // 2) == 0
    top = lax.rem(tile, tiles // 2) == tiles // 2 - 1

    def peer(d):
        return lax.rem(func + d, funcs)

    barrier = pltpu.get_barrier_semaphore()
    for d in range(1, funcs):
        pl.semaphore_signal(barrier, inc=1, device_id=(tile, peer(d)), device_id_type=MESH)
    pl.semaphore_signal(barrier, inc=1, device_id=(down, func), device_id_type=MESH)

    @pl.when(jnp.logical_not(top))
    def _():
        pl.semaphore_signal(barrier, inc=1, device_id=(up, func), device_id_type=MESH)


    mine = EDGE // 2 + func
    own_state = [pltpu.make_async_copy(chk.at[s], st.at[s, :, pl.ds(2 * mine, 2), :], own_sem.at[1 + s]) for s in range(2)]
    for s in (1, 0):
        own_state[s].start()
    own_seeds = pltpu.make_async_copy(seeds, adj.at[:, :, pl.ds(EDGE, 32), :], own_sem.at[0])
    own_seeds.start()
    mat[...] = y_matrix().astype(jnp.bfloat16)
    pl.semaphore_wait(barrier, funcs + 1 - bottom.astype(jnp.int32))

    @pl.when(top)
    def _():
        pl.semaphore_signal(entered, inc=1, device_id=(up, func), device_id_type=MESH)

    gather = [
        [
            pltpu.make_async_remote_copy(
                src_ref=chk.at[s],
                dst_ref=st.at[s, :, pl.ds(2 * mine, 2), :],
                send_sem=g_send.at[s, d],
                recv_sem=g_recv.at[s, d],
                device_id=(tile, peer(d)),
                device_id_type=MESH,
            )
            for d in range(1, funcs)
        ]
        for s in range(2)
    ]

    def across(src, dst, slot, to):
        return pltpu.make_async_remote_copy(
            src_ref=src, dst_ref=dst, send_sem=z_send.at[slot], recv_sem=z_recv.at[slot],
            device_id=(to, func), device_id_type=MESH,
        )

    lo, hi = EDGE // 2, EDGE // 2 + 16
    rims = [
        (
            across(st.at[s, :, pl.ds(2 * (hi - n), 2 * n), :], st.at[s, :, pl.ds(2 * (lo - n), 2 * n), :], 2 + 2 * s, up),
            across(st.at[s, :, pl.ds(2 * lo, 2 * n), :], st.at[s, :, pl.ds(2 * hi, 2 * n), :], 3 + 2 * s, down),
        )
        for s, n in enumerate((DEEP[0] // 2, DEEP[1] // 2))
    ]
    halo = (
        across(seeds.at[:, :, pl.ds(16, 16), :], adj.at[:, :, pl.ds(EDGE - 16, 16), :], 0, up),
        across(seeds.at[:, :, pl.ds(0, 16), :], adj.at[:, :, pl.ds(EDGE + 32, 16), :], 1, down),
    )
    for d in sorted(range(1, funcs), key=lambda d: -min(d, funcs - d)):
        gather[1][d - 1].start()

    def launch(pair):
        pair[0].start()

        @pl.when(jnp.logical_not(bottom))
        def _():
            pair[1].start()

    launch(halo)

    def relay(s):
        own_state[s].wait()
        for copy in gather[s]:
            copy.wait_recv()
        launch(rims[s])

    relay(1)
    for copy in gather[0]:
        copy.start()
    own_seeds.wait()

    def load(s):
        return lambda c, row: st[s, c, rowsat(row), :]

    def part(g, carry):
        above = (g == 0) != top

        def arrive(pair):
            @pl.when(above)
            def _():
                pair[1].wait_recv()

            @pl.when(jnp.logical_not(above))
            def _():
                pair[0].wait_recv()

        def region(deep, rim):
            first, last = -deep, 32 + deep
            low = jnp.where(top, jnp.where(g == 0, first, 32 - rim), jnp.where(g == 0, rim, first))
            high = jnp.where(top, jnp.where(g == 0, 32 - rim, last), jnp.where(g == 0, last, rim))
            return EDGE + low, EDGE + high

        def sections(s):
            return lambda k: region(DEEP[s] - 2 * k, 2 * k)

        def stages(first):
            return lambda place: region(16 - 2 * (first + place), 4 + 2 * (first + place))

        arrive(rims[1])
        forward(load(1), fx[1], base[1], coef[1], sections(1))

        @pl.when(g == 0)
        def _():
            relay(0)

        arrive(halo)

        def keep(f, c, row, v):
            fields[4][f, c, rowsat(row), :] = v

        backward(*fields[0:4], coef[1], stages(1), keep, mat)
        arrive(rims[0])
        forward(load(0), fx[0], base[0], coef[0], sections(0))

        def finish(f, c, row, v):
            out[f, c, pl.ds(row - EDGE, 8), :] = v

        backward(*fields[4:8], coef[0], stages(5), finish, mat)

        @pl.when(jnp.logical_and(g == 0, bottom))
        def _():
            pl.semaphore_wait(entered, 1)
            for pair in (halo, rims[1], rims[0]):
                pair[1].start()

        return carry

    lax.fori_loop(0, 2, part, 0)
    for copies in (*gather, halo, *rims):
        for copy in copies:
            copy.wait_send()


def solution(mesh):
    tiles, funcs = mesh.shape["tile"], mesh.shape["func"]

    def local(seeds, checkpoints):
        state = pltpu.VMEM((5, ROWS, L), jnp.float32)
        field = pltpu.VMEM((3, 5, ROWS, L), jnp.float32)
        return pl.pallas_call(
            functools.partial(kernel, tiles, funcs),
            out_shape=jax.ShapeDtypeStruct(seeds.shape, jnp.float32),
            in_specs=[pl.BlockSpec(memory_space=pltpu.HBM)] * 2,
            out_specs=pl.BlockSpec(memory_space=pltpu.VMEM),
            scratch_shapes=[state] * 12
            + [pltpu.VMEM((4, 5, ROWS, L), jnp.float32)] * 2
            + [field] * 8
            + [
                pltpu.VMEM((2, 5, ROWS, L), jnp.float32),
                pltpu.SemaphoreType.DMA((3,)),
                pltpu.SemaphoreType.DMA((2, 16)),
                pltpu.SemaphoreType.DMA((2, 16)),
                pltpu.SemaphoreType.DMA((6,)),
                pltpu.SemaphoreType.DMA((6,)),
                pltpu.SemaphoreType.REGULAR,
                pltpu.VMEM((L, L), jnp.bfloat16),
            ],
            compiler_params=pltpu.CompilerParams(
                collective_id=0, has_side_effects=True, vmem_limit_bytes=16 * 2**20
            ),
        )(seeds, checkpoints)

    return jax.shard_map(
        local,
        mesh=mesh,
        in_specs=(P("func", None, "tile", None), P(None, None, ("tile", "func"), None)),
        out_specs=P("func", None, "tile", None),
        check_vma=False,
    )
```
